128 devices in a mesh: shard: 32 (over z, x, core), tensor: 4 (over y).
Axes of the slice: x: 4, y: 4, z: 4, core: 2. Of those that a mesh axis runs over, the one named last changes fastest.
Arguments:
- gradients: bfloat16 [3, 1152, 6912], P(None, 'shard', 'tensor'), may hold values from -6 to 6
- weights: float32 [3, 1152, 6912], P(None, 'shard', 'tensor'), may hold values from -6 to 6
- projectors: bfloat16 [1152, 3, 256], replicated, may hold values from -0.1875 to 0.1875
- first_moment: float32 [3, 256, 4, 1728], P(None, None, 'tensor', 'shard'), may hold values from -3 to 3
- second_moment: float32 [3, 256, 4, 1728], P(None, None, 'tensor', 'shard'), may hold values from 0.05 to 4
Outputs:
- new_weight: float32 [3, 1152, 6912], P(None, 'shard', 'tensor')
- new_first: float32 [3, 256, 4, 1728], P(None, None, 'tensor', 'shard')
- new_second: float32 [3, 256, 4, 1728], P(None, None, 'tensor', 'shard')
- new_basis: bfloat16 [1152, 3, 256], replicated
The draws below stay inside these ranges and needn't reach their ends.
All inputs are finite; a program needn't handle non-finite values.
Results may differ from the reference program's by a relative error of at most 0.001.
The reference program's roundings to bfloat16 on the way (of `update` and `back`) count: a program that leaves them out, or rounds other values in their place, can miss the bound.
Values may be sent and summed in bfloat16 or wider, within the bound.
A program may use at most 64 MiB of HBM per device.

```python
import math
import jax
import jax.numpy as jnp
from jax import lax

D = 1152
FF = 6912
R = 256
MATS = 3
NS_STEPS = 5
N_TENSOR = 4


def level_of(own_key, shape, split, smallest, high):
    gain, own = 1.0, jax.random.fold_in(own_key, 6)
    for position, parts in split:
        draws = jnp.exp(jax.random.uniform(jax.random.fold_in(own, position), (parts,), jnp.float32, smallest / len(split), high / len(split)))
        gain = gain * jnp.repeat(draws, shape[position] // parts).reshape([-1 if axis == position else 1 for axis in range(len(shape))])
    return gain


def bell_draw(rng, shape, width, bound, shards=(), kind=jnp.bfloat16):
    gain = level_of(rng, shape, shards, -0.22, 0.18) if shards else 1.0
    drawn = jax.random.normal(rng, shape, jnp.float32) * width * gain
    return jnp.minimum(jnp.maximum(drawn, -bound), bound).astype(kind)


def setup_inputs(seed: int = 0) -> dict:
    splits = jax.random.split(jax.random.key(seed), 6)
    return {
        "gradients": bell_draw(splits[0], (MATS, D, FF), 1.0, 6.0, ((1, 32), (2, 4))),
        "weights": bell_draw(splits[1], (MATS, D, FF), 1.0, 6.0, ((1, 32), (2, 4)), jnp.float32),
        "projectors": bell_draw(splits[2], (D, MATS, R), D ** -0.5, 0.1875),
        "first_moment": bell_draw(splits[3], (MATS, R, N_TENSOR, FF // N_TENSOR), 0.3, 3.0, ((2, 4), (3, 32)), jnp.float32),
        "second_moment": jnp.clip(jnp.exp(math.log(4.0) - 4.3820266 * jax.random.uniform(splits[4], (MATS, R, N_TENSOR, FF // N_TENSOR), jnp.float32) ** level_of(splits[4], (MATS, R, N_TENSOR, FF // N_TENSOR), ((2, 4), (3, 32)), -0.2, 0.2)), 0.05, 4.0),
    }


corr_first = 1.0
corr_second = 0.6323045752

def reference(gradients, weights, projectors, first_moment, second_moment):
    first_whole = first_moment.reshape(MATS, R, FF)
    second_whole = second_moment.reshape(MATS, R, FF)
    weight_list = []
    first_list = []
    second_list = []
    basis_list = []
    for index in range(MATS):
        grad_mat = gradients[index]
        basis_mat = projectors[:, index, :]
        projected = jnp.dot(basis_mat.T, grad_mat, preferred_element_type=jnp.float32)
        first_new = 0.9 * first_whole[index] + 0.1 * projected
        second_new = 0.999 * second_whole[index] + 0.001 * projected * projected
        update = (first_new / corr_first / (jnp.sqrt(second_new / corr_second) + 1e-08)).astype(jnp.bfloat16)
        delta = jnp.dot(basis_mat, update, preferred_element_type=jnp.float32)
        weight_list.append(weights[index] - 0.2 * delta)
        first_list.append(first_new)
        second_list.append(second_new)
        back = jnp.dot(grad_mat.T, basis_mat, preferred_element_type=jnp.float32).astype(jnp.bfloat16)
        refresh = jnp.dot(grad_mat, back, preferred_element_type=jnp.float32)
        iterate = refresh / jnp.sqrt(jnp.sum(refresh * refresh) + 1e-06)
        for sweep in range(NS_STEPS):
            inner = jnp.dot(iterate.T, iterate, precision=lax.Precision.HIGHEST, preferred_element_type=jnp.float32)
            iterate = 1.5 * iterate - 0.5 * jnp.dot(iterate, inner, precision=lax.Precision.HIGHEST, preferred_element_type=jnp.float32)
        basis_list.append((iterate * math.sqrt(D)).astype(jnp.bfloat16))
    shape_four = (MATS, R, N_TENSOR, FF // N_TENSOR)
    return (jnp.stack(weight_list), jnp.stack(first_list).reshape(shape_four), jnp.stack(second_list).reshape(shape_four), jnp.stack(basis_list, axis=1))
```

```python
import functools
import math

import jax
import jax.numpy as jnp
from jax import lax
from jax.experimental import pallas as pl
from jax.experimental.pallas import tpu as pltpu
from jax.sharding import PartitionSpec as P

MESH = pl.DeviceIdType.MESH
F32, BF16 = jnp.float32, jnp.bfloat16
NS_STEPS = 5
CORR_FIRST = 1.0
CORR_SECOND = 0.6323045752
ROWS, COLS = 36, 54
PADR = 48
SLOT = 64
ROW40 = 40
NDEV, NCHIP = 32, 16


def dot(a, b):
    return jnp.dot(a, b, preferred_element_type=F32)


def dot_nt(a, b):
    return lax.dot_general(a, b, (((1,), (1,)), ((), ())), preferred_element_type=F32)


def split(a):
    hi = a.astype(BF16)
    return hi, (a - hi.astype(F32)).astype(BF16)


def dot3(a, b):
    ah, al = split(a)
    bh, bl = split(b)
    return dot(ah, bh) + (dot(ah, bl) + dot(al, bh))


class Gather:
    def __init__(self, buf, quarter, send_sem, recv_sem, where, own_to_sibling):
        self.buf, self.q, self.ssem, self.rsem = buf, quarter, send_sem, recv_sem
        self.z, self.x, self.k, self.y = where
        self.own = own_to_sibling
        self.started = []
        self.keys = {}

    @staticmethod
    def n_sems():
        return 2 * (2 + 2 + 8 + 8 + 16)

    def key(self, key):
        return self.keys.setdefault(key, len(self.keys))

    def chip(self, h, o1, o2):
        ox, oz = (o1, o2) if h == 0 else (o2, o1)
        return lax.rem(self.z + oz, 4) * 4 + lax.rem(self.x + ox, 4)

    def view(self, h, o1, o2, part, core):
        slot = self.chip(h, o1, o2) * 2 + core
        if part is None:
            rows = pl.ds(2 * h * self.q, 2 * self.q)
        else:
            rows = pl.ds((2 * h + part) * self.q, self.q)
        return self.buf.at[slot, rows, :]

    def copy(self, view, ssem, rsem, shard):
        return pltpu.make_async_remote_copy(
            src_ref=view, dst_ref=view, send_sem=self.ssem.at[ssem], recv_sem=self.rsem.at[rsem],
            device_id=(shard, self.y), device_id_type=MESH)

    def send(self, h, o1, o2, part, axis, step):
        d1, d2 = (step, 0) if axis == 1 else (0, step)
        shard = self.chip(h, d1 % 4, d2 % 4) * 2 + self.k
        there = (h, (o1 - d1) % 4, (o2 - d2) % 4, part)
        c = self.copy(self.view(h, o1, o2, part, self.k), len(self.started), self.key(there), shard)
        c.start()
        self.started.append(c)

    def wait(self, h, o1, o2, part):
        shard = self.chip(h, 0, 0) * 2 + 1 - self.k
        self.copy(self.view(h, o1, o2, part, self.k), 0, self.key((h, o1, o2, part)), shard).wait_recv()

    def sib(self, h, o1, o2):
        shard = self.chip(h, 0, 0) * 2 + 1 - self.k
        c = self.copy(self.view(h, o1, o2, None, self.k), len(self.started), self.key(("s", h, o1, o2)), shard)
        c.start()
        self.started.append(c)

    def wait_sib(self, h, o1, o2):
        shard = self.chip(h, 0, 0) * 2 + 1 - self.k
        self.copy(self.view(h, o1, o2, None, 1 - self.k), 0, self.key(("s", h, o1, o2)), shard).wait_recv()

    def stages(self):
        halves = (0, 1)
        for h in halves:
            for axis in (1, 2):
                for step in (1, -1):
                    self.send(h, 0, 0, None, axis, step)
            if self.own:
                self.sib(h, 0, 0)
        yield
        for o1 in (3, 1):
            for h in halves:
                self.wait(h, o1, 0, None)
                self.send(h, o1, 0, 0 if o1 == 3 else 1, 1, 1 if o1 == 3 else -1)
                self.send(h, o1, 0, None, 2, 1)
                self.send(h, o1, 0, None, 2, -1)
                self.sib(h, o1, 0)
        yield
        for o2 in (3, 1):
            for h in halves:
                self.wait(h, 0, o2, None)
                self.send(h, 0, o2, 0 if o2 == 3 else 1, 2, 1 if o2 == 3 else -1)
                self.sib(h, 0, o2)
        yield
        for h in halves:
            self.wait(h, 2, 0, 0)
            self.wait(h, 2, 0, 1)
            self.send(h, 2, 0, None, 2, 1)
            self.send(h, 2, 0, None, 2, -1)
            self.sib(h, 2, 0)
        yield
        for o1 in (3, 1, 2):
            for o2 in (3, 1):
                for h in halves:
                    self.wait(h, o1, o2, None)
                    self.send(h, o1, o2, 0 if o2 == 3 else 1, 2, 1 if o2 == 3 else -1)
                    self.sib(h, o1, o2)
        yield
        for o1 in (0, 3, 1, 2):
            for h in halves:
                self.wait(h, o1, 2, 0)
                self.wait(h, o1, 2, 1)
                self.sib(h, o1, 2)
        yield
        for o1 in range(4):
            for o2 in range(4):
                if (o1, o2) != (0, 0) or self.own:
                    for h in halves:
                        self.wait_sib(h, o1, o2)
        yield

    def drain(self):
        for c in self.started:
            c.wait_send()


def kernel(factor, g_ref, p_ref, m1_ref, m2_ref, delta_ref, nf_ref, ns_ref, basis_ref,
           sbuf, rbuf, ppad, pt, tbuf, bbuf, ubuf, ybuf, xbuf, xh, xl,
           a_send, a_recv, f_send, f_recv, y_send, y_recv, b_send, b_recv, x_send, x_recv, u_send, u_recv):
    s = lax.axis_index("shard")
    y = lax.axis_index("tensor")
    c = s // 2
    k = s % 2
    z, x = c // 4, c % 4
    sibling = c * 2 + 1 - k
    mats = g_ref.shape[0]
    rank = p_ref.shape[2]

    barrier = pltpu.get_barrier_semaphore()
    for j in range(1, NCHIP):
        pl.semaphore_signal(barrier, inc=1, device_id=(lax.rem(c + j, NCHIP) * 2 + k, y), device_id_type=MESH)
    pl.semaphore_signal(barrier, inc=1, device_id=(sibling, y), device_id_type=MESH)
    for j in range(1, 4):
        pl.semaphore_signal(barrier, inc=1, device_id=(s, lax.rem(y + j, 4)), device_id_type=MESH)

    sbuf[...] = jnp.zeros_like(sbuf)
    for t in range(NDEV):
        sbuf[t // 2, :, 0:ROWS, SLOT * (t % 2):SLOT * (t % 2) + COLS] = g_ref[:, :, COLS * t:COLS * t + COLS]
    pl.semaphore_wait(barrier, NCHIP - 1 + 1 + 3)

    def piece(j, core):
        return rbuf.at[:, lax.rem(c + NCHIP - j, NCHIP) * 2 + core]

    def to_chip(j):
        return pltpu.make_async_remote_copy(
            src_ref=sbuf.at[lax.rem(c + j, NCHIP)], dst_ref=rbuf.at[:, s], send_sem=a_send.at[j], recv_sem=a_recv.at[j],
            device_id=(lax.rem(c + j, NCHIP) * 2 + k, y), device_id_type=MESH)

    def to_sibling(j, core):
        return pltpu.make_async_remote_copy(
            src_ref=sbuf.at[c] if j == 0 else piece(j, core), dst_ref=piece(j, core), send_sem=f_send.at[j],
            recv_sem=f_recv.at[j], device_id=(sibling, y), device_id_type=MESH)

    order = [4, 12, 1, 15, 3, 13, 5, 11, 8, 2, 14, 7, 9, 6, 10]
    for j in order:
        to_chip(j).start()
    to_sibling(0, k).start()
    rbuf[:, s] = sbuf[c]

    ppad[...] = jnp.zeros_like(ppad)
    for t in range(NDEV):
        ppad[:, PADR * t:PADR * t + ROWS, :] = p_ref[:, ROWS * t:ROWS * t + ROWS, :]
    for m in range(mats):
        for t in range(NDEV * PADR // 256):
            pt[m, :, 256 * t:256 * t + 256] = ppad[m, 256 * t:256 * t + 256, :].T

    def arrived(j, core):
        pltpu.make_async_remote_copy(
            src_ref=piece(j, core), dst_ref=piece(j, core), send_sem=a_send.at[j], recv_sem=a_recv.at[j],
            device_id=(sibling, y), device_id_type=MESH).wait_recv()

    for j in order:
        arrived(j, k)
        to_sibling(j, k).start()
    for j in [0] + order:
        pltpu.make_async_remote_copy(
            src_ref=piece(j, 1 - k), dst_ref=piece(j, 1 - k), send_sem=f_send.at[j], recv_sem=f_recv.at[j],
            device_id=(sibling, y), device_id_type=MESH).wait_recv()

    for m in range(mats):
        cols = slice(rank * m, rank * m + rank)
        projected = dot(pt[m], rbuf[m].reshape(NDEV * PADR, 2 * SLOT)).T
        tbuf[m] = projected
        bbuf[2 * c, :, cols] = projected[:SLOT].astype(BF16)
        bbuf[2 * c + 1, :, cols] = projected[SLOT:].astype(BF16)

    where = (z, x, k, y)
    gather_back = Gather(bbuf, SLOT // 4, b_send, b_recv, where, False)
    gather_rows = Gather(xbuf, 32, x_send, x_recv, where, True)
    gather_update = Gather(ubuf, SLOT // 4, u_send, u_recv, where, True)
    stages = gather_back.stages()
    next(stages)

    ubuf[s] = jnp.zeros((SLOT, mats * rank), BF16)
    for m in range(mats):
        own = tbuf[m, pl.ds(pl.multiple_of(SLOT * k, SLOT), SLOT), :][:COLS]
        first = 0.9 * m1_ref[m] + 0.1 * own
        second = 0.999 * m2_ref[m] + 0.001 * own * own
        nf_ref[m] = first
        ns_ref[m] = second
        update = first / CORR_FIRST / (jnp.sqrt(second / CORR_SECOND) + 1e-08)
        ubuf[s, 0:COLS, rank * m:rank * m + rank] = update.astype(BF16)
    for _ in stages:
        pass

    ybuf[y, 96:128, :] = jnp.zeros((32, rank), F32)
    for m in range(mats):
        total = None
        for i in range(NCHIP // 2):
            lhs = jnp.concatenate([sbuf[2 * i, m], sbuf[2 * i + 1, m]], axis=1)
            rhs = bbuf[4 * i:4 * i + 4, :, rank * m:rank * m + rank].reshape(4 * SLOT, rank)
            term = dot(lhs, rhs)
            total = term if total is None else total + term
        ybuf[y, ROW40 * m:ROW40 * m + ROW40, :] = total[:ROW40]

    def to_tensor(j, slot):
        return pltpu.make_async_remote_copy(
            src_ref=ybuf.at[slot], dst_ref=ybuf.at[slot], send_sem=y_send.at[j], recv_sem=y_recv.at[j],
            device_id=(s, lax.rem(y + j, 4)), device_id_type=MESH)

    for j in (1, 3, 2):
        to_tensor(j, y).start()
    for j in (1, 3, 2):
        to_tensor(j, lax.rem(y + 4 - j, 4)).wait_recv()
    xbuf[s] = ((ybuf[0] + ybuf[1]) + ybuf[2]) + ybuf[3]
    for _ in gather_rows.stages():
        pass

    stages = gather_update.stages()
    next(stages)
    row = lax.broadcasted_iota(jnp.int32, (rank, rank), 0)
    eye = jnp.where(row == lax.broadcasted_iota(jnp.int32, (rank, rank), 1), 1.0, 0.0).astype(F32)
    grams, scales = [], []
    for m in range(mats):
        hi, lo = split(xbuf[:, ROW40 * m:ROW40 * m + ROW40, :].reshape(NDEV * ROW40, rank))
        xh[m] = hi
        xl[m] = lo
        hi_t = hi.T
        cross = dot(hi_t, lo)
        raw = dot(hi_t, hi) + (cross + cross.T)
        square = jnp.sum(raw * eye, keepdims=True) + 1e-06
        scales.append(factor / jnp.sqrt(square))
        grams.append(raw / square)
    next(stages)
    q = [None] * mats
    for sweep in range(NS_STEPS):
        for m in range(mats):
            step = 1.5 * eye - 0.5 * grams[m]
            if sweep < NS_STEPS - 1:
                grams[m] = dot3(dot3(grams[m], step), step)
            q[m] = step if sweep == 0 else dot3(q[m], step)
        next(stages)
    for _ in stages:
        pass
    for m in range(mats):
        qh, ql = split(q[m])
        iterate = dot(xh[m], qh) + (dot(xh[m], ql) + dot(xl[m], qh))
        basis_ref[m] = (iterate * scales[m]).astype(BF16)

    for m in range(mats):
        rows = ppad[m, pl.ds(pl.multiple_of(PADR * s, 16), PADR), :]
        for i in range(NDEV // 4):
            cols = ubuf[4 * i:4 * i + 4, :, rank * m:rank * m + rank].reshape(4 * SLOT, rank)
            part = dot_nt(rows, cols)
            for t in range(4):
                start = COLS * (4 * i + t)
                delta_ref[m, :, start:start + COLS] = part[:ROWS, SLOT * t:SLOT * t + COLS]

    for j in order:
        to_chip(j).wait_send()
    for j in [0] + order:
        to_sibling(j, k).wait_send()
    for j in (1, 3, 2):
        to_tensor(j, y).wait_send()
    for g in (gather_back, gather_rows, gather_update):
        g.drain()


def per_device(gradients, weights, projectors, first_moment, second_moment):
    width, mats, rank = projectors.shape
    _, rows, cols = gradients.shape
    hidden = first_moment.shape[3]
    planes = jnp.transpose(projectors, (1, 0, 2))
    m1 = jnp.transpose(first_moment.reshape(mats, rank, hidden), (0, 2, 1))
    m2 = jnp.transpose(second_moment.reshape(mats, rank, hidden), (0, 2, 1))
    vmem = pl.BlockSpec(memory_space=pltpu.VMEM)
    dma = lambda n: pltpu.SemaphoreType.DMA((n,))
    n = Gather.n_sems()
    delta, first, second, basis = pl.pallas_call(
        functools.partial(kernel, math.sqrt(width)),
        out_shape=(
            jax.ShapeDtypeStruct((mats, rows, cols), F32),
            jax.ShapeDtypeStruct((mats, hidden, rank), F32),
            jax.ShapeDtypeStruct((mats, hidden, rank), F32),
            jax.ShapeDtypeStruct((mats, NDEV * ROW40, rank), BF16),
        ),
        in_specs=[vmem] * 4,
        out_specs=(vmem,) * 4,
        scratch_shapes=[
            pltpu.VMEM((NCHIP, mats, PADR, 2 * SLOT), BF16),
            pltpu.VMEM((mats, NDEV, PADR, 2 * SLOT), BF16),
            pltpu.VMEM((mats, NDEV * PADR, rank), BF16),
            pltpu.VMEM((mats, rank, NDEV * PADR), BF16),
            pltpu.VMEM((mats, 2 * SLOT, rank), F32),
            pltpu.VMEM((NDEV, SLOT, mats * rank), BF16),
            pltpu.VMEM((NDEV, SLOT, mats * rank), BF16),
            pltpu.VMEM((4, 128, rank), F32),
            pltpu.VMEM((NDEV, 128, rank), F32),
            pltpu.VMEM((mats, NDEV * ROW40, rank), BF16),
            pltpu.VMEM((mats, NDEV * ROW40, rank), BF16),
            dma(NCHIP), dma(NCHIP), dma(NCHIP), dma(NCHIP), dma(4), dma(4),
            dma(n), dma(n), dma(n), dma(n), dma(n), dma(n),
        ],
        compiler_params=pltpu.CompilerParams(
            collective_id=0, has_side_effects=True, vmem_limit_bytes=60 * 1024 * 1024),
    )(gradients, planes, m1, m2)
    new_weight = weights - 0.2 * delta
    shape_four = first_moment.shape
    first = jnp.transpose(first, (0, 2, 1)).reshape(shape_four)
    second = jnp.transpose(second, (0, 2, 1)).reshape(shape_four)
    basis = basis.reshape(mats, NDEV, ROW40, rank)[:, :, :rows].reshape(mats, width, rank)
    return new_weight, first, second, jnp.transpose(basis, (1, 0, 2))


def solution(mesh):
    in_specs = (
        P(None, "shard", "tensor"),
        P(None, "shard", "tensor"),
        P(),
        P(None, None, "tensor", "shard"),
        P(None, None, "tensor", "shard"),
    )
    out_specs = (
        P(None, "shard", "tensor"),
        P(None, None, "tensor", "shard"),
        P(None, None, "tensor", "shard"),
        P(),
    )
    return jax.shard_map(
        per_device, mesh=mesh, in_specs=in_specs, out_specs=out_specs, check_vma=False
    )
```
